32 devices in a mesh: depth: 8 (over y, x, core), rows: 4 (over z).
Axes of the slice: x: 2, y: 2, z: 4, core: 2. Of those that a mesh axis runs over, the one named last changes fastest.
Arguments:
- ref_feat: bfloat16 [2, 8, 5120], P(None, 'rows'), may hold values from -6 to 6
- src_feat: bfloat16 [2, 4, 8, 5120], P(None, None, 'rows'), may hold values from -6 to 6
- block_index: int32 [2, 4, 48, 4], P(None, None, 'depth', 'rows'), may hold values from 0 to 2, as said below
- blend: bfloat16 [2, 4, 48, 8, 160], P(None, None, 'depth', 'rows'), may hold values from 0 to 1
- conv_first: bfloat16 [3, 3, 3, 32, 40], replicated, may hold values from -0.1875 to 0.1875
- bias_first: float32 [32], replicated, may hold values from -3 to 3
- conv_second: bfloat16 [3, 3, 3, 32, 32], replicated, may hold values from -0.21875 to 0.21875
- bias_second: float32 [32], replicated, may hold values from -3 to 3
Outputs:
- regularized: bfloat16 [2, 48, 8, 5120], P(None, 'depth', 'rows')
The draws below stay inside these ranges and needn't reach their ends.
Inputs may be any that keep to these rules, and one draw needn't show every extreme that they name: block_index[b, v, d, q] is q - 1 or q, held within 0 to 2, so rows of block q blend source row blocks block_index and block_index + 1.
All inputs are finite; a program needn't handle non-finite values.
Results may differ from the reference program's by a relative error of at most 0.0046.
Values may be sent and summed in bfloat16 or wider, within the bound.
A program may use at most 64 MiB of HBM per device.

```python
import jax
import jax.numpy as jnp
from jax import lax

FEAT = 32
GROUPS = 8
REG = 32
SRC = 4
WIDTH = 160
ROWS_DEV = 2
BATCH = 2
D = 48
H = 8
NB = 4


def draw_block_index(key, part):
    offset = jax.random.randint(key, (BATCH, SRC, D, NB), -1, 1, dtype=jnp.int32)
    blocks = jnp.arange(NB, dtype=jnp.int32)
    return jnp.clip(blocks + offset, 0, NB - 2).astype(jnp.int32)


def steps_of(key, extent, cuts, least, top_value):
    loudness = 1.0
    for dim, blocks in cuts:
        heights = jax.random.uniform(jax.random.fold_in(jax.random.fold_in(key, 6), dim), (blocks,), jnp.float32, least / len(cuts), top_value / len(cuts))
        loudness = loudness * jnp.repeat(jnp.exp(heights), extent[dim] // blocks).reshape((-1,) + (1,) * (len(extent) - 1 - dim))
    return loudness


def bell_draw(own_key, shape, deviation, bound, shards=(), held_as=jnp.bfloat16):
    drawn = deviation * jax.random.normal(own_key, shape, jnp.float32)
    if shards:
        drawn = drawn * steps_of(own_key, shape, shards, -0.22, 0.18)
    return jnp.clip(drawn, -bound, bound).astype(held_as)


def setup_inputs(seed: int = 0) -> dict:
    splits = jax.random.split(jax.random.key(seed), 9)
    return {
        "ref_feat": bell_draw(splits[0], (BATCH, H, FEAT * WIDTH), 1.0, 6.0, ((1, 4),)),
        "src_feat": bell_draw(splits[1], (BATCH, SRC, H, FEAT * WIDTH), 1.0, 6.0, ((2, 4),)),
        "block_index": draw_block_index(jax.random.fold_in(splits[8], 71), 0),
        "blend": jnp.clip(1.0 * jax.random.uniform(splits[3], (BATCH, SRC, D, H, WIDTH), jnp.float32) ** steps_of(splits[3], (BATCH, SRC, D, H, WIDTH), ((2, 8), (3, 4)), -0.2, 0.2), 0.0, 1.0).astype(jnp.bfloat16),
        "conv_first": bell_draw(splits[4], (3, 3, 3, REG, GROUPS + FEAT), (27 * (GROUPS + FEAT)) ** -0.5, 0.1875),
        "bias_first": bell_draw(splits[5], (REG,), 0.5, 3.0, (), jnp.float32),
        "conv_second": bell_draw(splits[6], (3, 3, 3, REG, REG), (27 * REG) ** -0.5, 0.21875),
        "bias_second": bell_draw(splits[7], (REG,), 0.5, 3.0, (), jnp.float32),
    }


def cost_plane(ref_rows, top_rows, bottom_rows, weight, feat_count, columns, groups):
    scenes = top_rows.shape[0]
    source_views = top_rows.shape[1]
    row_count = top_rows.shape[2]
    reference_cube = ref_rows.astype(jnp.float32).reshape(scenes, 1, row_count, feat_count, columns)
    blend_weight = weight.astype(jnp.float32)[:, :, :, None, :]
    upper_part = top_rows.astype(jnp.float32).reshape(scenes, source_views, row_count, feat_count, columns)
    lower_part = bottom_rows.astype(jnp.float32).reshape(scenes, source_views, row_count, feat_count, columns)
    warped = blend_weight * upper_part + (1.0 - blend_weight) * lower_part
    average = (reference_cube[:, 0] + jnp.sum(warped, axis=1)) / (source_views + 1.0)
    spread = ((reference_cube[:, 0] - average) ** 2 + jnp.sum((warped - average[:, None]) ** 2, axis=1)) / (source_views + 1.0)
    per_group = feat_count // groups
    products = (reference_cube * warped).reshape(scenes, source_views, row_count, groups, per_group, columns)
    correlation = jnp.sum(products, axis=(1, 4)) / (source_views * per_group * 1.0)
    stacked = jnp.concatenate([correlation, spread], axis=2).astype(jnp.bfloat16)
    return stacked.reshape(scenes, row_count, (groups + feat_count) * columns)


def layer(volume, kernel, shift_bias, rectify):
    scenes = volume.shape[0]
    channels = kernel.shape[4]
    outputs = kernel.shape[3]
    shaped = volume.reshape(scenes, D, H, channels, WIDTH)
    padded = jnp.pad(shaped, ((0, 0), (1, 1), (1, 1), (0, 0), (1, 1)))
    kernel_wide = kernel.astype(jnp.float32)

    def one_plane(plane):
        block = lax.dynamic_slice_in_dim(padded, plane, 3, 1).astype(jnp.float32)
        summed = jnp.zeros((scenes, H, outputs, WIDTH), jnp.float32)
        for tap_depth in range(3):
            for tap_row in range(3):
                for tap_col in range(3):
                    piece = block[:, tap_depth, tap_row:tap_row + H, :, tap_col:tap_col + WIDTH]
                    summed = summed + jnp.einsum("brcw,oc->brow", piece, kernel_wide[tap_depth, tap_row, tap_col], precision=lax.Precision.HIGHEST)
        result = summed + shift_bias.astype(jnp.float32)[None, None, :, None]
        if rectify:
            result = jnp.maximum(result, 0.0)
        return result.astype(jnp.bfloat16).reshape(scenes, H, outputs * WIDTH)

    planes_out = lax.map(one_plane, jnp.arange(D, dtype=jnp.int32))
    return jnp.moveaxis(planes_out, 0, 1)


def reference(ref_feat, src_feat, block_index, blend, conv_first, bias_first, conv_second, bias_second):
    row_block = jnp.arange(H, dtype=jnp.int32) // ROWS_DEV
    within = jnp.arange(H, dtype=jnp.int32) % ROWS_DEV

    def plane_cost(plane):
        chosen = lax.dynamic_index_in_dim(block_index, plane, 2, keepdims=False)[:, :, row_block]
        top_index = (chosen * ROWS_DEV + within).astype(jnp.int32)[..., None]
        bottom_index = (top_index + ROWS_DEV).astype(jnp.int32)
        top_rows = jnp.take_along_axis(src_feat, top_index, axis=2)
        bottom_rows = jnp.take_along_axis(src_feat, bottom_index, axis=2)
        weight = lax.dynamic_index_in_dim(blend, plane, 2, keepdims=False)
        return cost_plane(ref_feat, top_rows, bottom_rows, weight, FEAT, WIDTH, GROUPS)

    cost_planes = lax.map(plane_cost, jnp.arange(D, dtype=jnp.int32))
    volume = jnp.moveaxis(cost_planes, 0, 1)
    hidden = layer(volume, conv_first, bias_first, True)
    return layer(hidden, conv_second, bias_second, False)
```

```python
import functools

import jax
import jax.numpy as jnp
from jax import lax
from jax.experimental import pallas as pl
from jax.experimental.pallas import tpu as pltpu
from jax.sharding import PartitionSpec as P

MESH = pl.DeviceIdType.MESH
LANES = 128
NEAR = ((0, 1), (0, -1), (1, 0), (-1, 0), (1, 1), (1, -1), (-1, 1), (-1, -1))
FAR = ((0, 2), (0, -2))


def kernel(
    dims, feat_in, coef_in, k1_in, b1_in, k2_in, b2_in, out_ref,
    feat, coef, vol, hid, work, w1, w2, prep, bias, send_sem, recv_sem, local_sem,
):
    scenes, views, rows, planes, feats, groups, columns, regs, depth_n, rows_n = dims
    channels = groups + feats
    per_group = feats // groups
    packed = feat_in.shape[3]
    wide = 2 * LANES
    tail = columns - LANES
    d = lax.axis_index("depth")
    q = lax.axis_index("rows")

    def exists(dd, dq):
        return (d + dd >= 0) & (d + dd < depth_n) & (q + dq >= 0) & (q + dq < rows_n)

    barrier = pltpu.get_barrier_semaphore()
    for dd, dq in NEAR + FAR:
        @pl.when(exists(dd, dq))
        def _():
            pl.semaphore_signal(barrier, inc=1, device_id=(d + dd, q + dq), device_id_type=MESH)

    local = [
        pltpu.make_async_copy(feat_in, feat.at[2], local_sem.at[0]),
        pltpu.make_async_copy(coef_in, coef.at[1, pl.ds(2, planes)], local_sem.at[1]),
    ]
    for copy in local:
        copy.start()

    def feat_copy(dq, k):
        slot = 2 - dq
        count = views + 1 if abs(dq) == 1 else views
        return pltpu.make_async_remote_copy(
            src_ref=feat_in.at[pl.ds(0, count)],
            dst_ref=feat.at[slot, pl.ds(0, count)],
            send_sem=send_sem.at[k], recv_sem=recv_sem.at[k],
            device_id=(d, q + dq), device_id_type=MESH,
        )

    def coef_copy(dd, dq, k):
        if dd == 0:
            first, count, at = 0, planes, 2
        elif dd == 1:
            first, count, at = planes - 2, 2, 0
        else:
            first, count, at = 0, 2, planes + 2
        return pltpu.make_async_remote_copy(
            src_ref=coef_in.at[pl.ds(first, count)],
            dst_ref=coef.at[1 - dq, pl.ds(at, count)],
            send_sem=send_sem.at[k], recv_sem=recv_sem.at[k],
            device_id=(d + dd, q + dq), device_id_type=MESH,
        )

    near_feat = [((0, dq), feat_copy(dq, i)) for i, dq in enumerate((1, -1))]
    far_feat = [((0, dq), feat_copy(dq, 2 + i)) for i, dq in enumerate((2, -2))]
    depth_coef = [((dd, 0), coef_copy(dd, 0, 4 + i)) for i, dd in enumerate((1, -1))]
    side_coef = [
        ((dd, dq), coef_copy(dd, dq, 6 + i))
        for i, (dd, dq) in enumerate([m for m in NEAR if m[1] != 0])
    ]
    every = depth_coef + near_feat + side_coef + far_feat

    for slot, gone in ((0, q < 2), (1, q < 1), (3, q + 1 >= rows_n), (4, q + 2 >= rows_n)):
        @pl.when(gone)
        def _():
            feat[slot] = jnp.zeros(feat.shape[1:], feat.dtype)

    beside = 1 + lax.div(d + depth_n - 1, depth_n) + lax.div(2 * depth_n - 2 - d, depth_n)
    above = 1 + lax.div(q + rows_n - 1, rows_n) + lax.div(2 * rows_n - 2 - q, rows_n)
    beyond = lax.div(q + rows_n - 2, rows_n) + lax.div(2 * rows_n - 3 - q, rows_n)
    pl.semaphore_wait(barrier, beside * above - 1 + beyond)

    for (dd, dq), copy in every:
        @pl.when(exists(dd, dq))
        def _():
            copy.start()

    def arrive(pairs):
        for (dd, dq), copy in pairs:
            @pl.when(exists(-dd, -dq))
            def _():
                copy.wait_recv()

    def place(kernel_in, count, span, target, dest):
        for a in range(3):
            for r in range(3):
                line = jnp.zeros((regs, span), jnp.float32)
                for s in range(3):
                    c = lax.broadcasted_iota(jnp.int32, (count, span), 0)
                    k = lax.broadcasted_iota(jnp.int32, (count, span), 1)
                    pick = jnp.where(dest(s, c) == k, 1.0, 0.0).astype(jnp.bfloat16)
                    line = line + jnp.dot(kernel_in[a, r, s], pick, preferred_element_type=jnp.float32)
                line = line.astype(jnp.bfloat16)
                for j in range(rows):
                    target[pl.ds((a * rows + j) * regs, regs), pl.ds((j + r) * span, span)] = line

    def first_dest(s, c):
        f = c - groups
        spread_at = s * feats + (f % per_group) * groups + f // per_group
        return jnp.where(c < groups, 3 * feats + s * groups + c, spread_at)

    w1[...] = jnp.zeros(w1.shape, w1.dtype)
    w2[...] = jnp.zeros(w2.shape, w2.dtype)
    place(k1_in, channels, LANES, w1, first_dest)
    place(k2_in, regs, LANES, w2, lambda s, c: s * regs + c)
    eye = lax.broadcasted_iota(jnp.int32, (regs, regs), 0) == lax.broadcasted_iota(
        jnp.int32, (regs, regs), 1
    )
    for i, b_in in enumerate((b1_in, b2_in)):
        column = jnp.sum(jnp.where(eye, b_in[...], 0.0), axis=1, keepdims=True)
        bias[i] = jnp.broadcast_to(jnp.concatenate([column] * rows, axis=0), (rows * regs, wide))

    for copy in local:
        copy.wait()

    lane = lax.broadcasted_iota(jnp.int32, (groups, LANES), 1)
    in_tail = lane < tail

    def unpack(tail_packed):
        parts = []
        for j in range(per_group):
            part = tail_packed if j == 0 else pltpu.roll(tail_packed, LANES - tail * j, 1)
            parts.append(jnp.where(in_tail, part, 0.0))
        return parts

    def volume_rows(block):
        for b in range(scenes):
            for m in range(rows):
                ref = feat[block + 1, views, b, m].astype(jnp.float32)
                prep[3 * views] = ref
                for v in range(views):
                    low = feat[block, v, b, m].astype(jnp.float32)
                    mid = feat[block + 1, v, b, m].astype(jnp.float32)
                    up = feat[block + 2, v, b, m].astype(jnp.float32)
                    prep[v] = mid - ref
                    prep[views + v] = low - mid
                    prep[2 * views + v] = up - mid
                row = (block - 1) * rows + m
                row_ok = (q * rows + row >= 0) & (q * rows + row < rows_n * rows)

                def plane(p, carry):
                    at = d * planes + p - 2
                    ok = row_ok & (at >= 0) & (at < depth_n * planes)
                    weights = coef[block, p, b, m].astype(jnp.float32)
                    others = 1.0 - weights
                    total = None
                    for v in range(views):
                        cl = weights[v : v + 1]
                        cu = others[views + v : views + v + 1]
                        both = []
                        for lo, hi, l0 in ((0, feats, 0), (feats, packed, LANES)):
                            both.append(
                                prep[v, lo:hi]
                                + cl[:, l0 : l0 + LANES] * prep[views + v, lo:hi]
                                + cu[:, l0 : l0 + LANES] * prep[2 * views + v, lo:hi]
                            )
                        if total is None:
                            total = both
                            square = [u * u for u in both]
                        else:
                            total = [t + u for t, u in zip(total, both)]
                            square = [t + u * u for t, u in zip(square, both)]
                    share = 1.0 / (views + 1.0)
                    spread = [(s2 - t * t * share) * share for s2, t in zip(square, total)]
                    refs = [prep[3 * views, 0:feats], prep[3 * views, feats:packed]]
                    product = [r * (t + (1.0 * views) * r) for r, t in zip(refs, total)]
                    scale = 1.0 / (views * per_group)
                    head = product[0][0:groups]
                    for j in range(1, per_group):
                        head = head + product[0][j * groups : (j + 1) * groups]
                    rest = product[1]
                    step = LANES // 2
                    while step >= tail:
                        rest = rest + pltpu.roll(rest, step, 1)
                        step //= 2
                    corr = jnp.concatenate([head, jnp.where(in_tail, rest, 0.0)], axis=1) * scale
                    ends = unpack(spread[1])
                    full = jnp.concatenate(
                        [jnp.concatenate([spread[0], jnp.concatenate(ends, axis=0)], axis=1), corr],
                        axis=0,
                    )
                    full = jnp.where(ok, full, 0.0)
                    left = pltpu.roll(full, 1, 1)
                    right = pltpu.roll(full, wide - 1, 1)
                    lines = [left[:feats], full[:feats], right[:feats]]
                    lines += [left[feats:], full[feats:], right[feats:]]
                    lines.append(jnp.zeros((LANES - 3 * channels, wide), jnp.float32))
                    vol[b, p, row + rows] = jnp.concatenate(lines, axis=0).astype(jnp.bfloat16)
                    return carry

                lax.fori_loop(0, planes + 4, plane, 0)

    arrive(depth_coef)
    arrive(near_feat)
    volume_rows(1)
    arrive(side_coef)
    arrive(far_feat)
    volume_rows(0)
    volume_rows(2)

    size = rows * regs
    inside = lax.broadcasted_iota(jnp.int32, (regs, wide), 1) < columns
    for b in range(scenes):
        for pair in range(2):
            base = pair * rows

            def first(p, carry):
                piece = vol[b, p, pl.ds(base, rows + 2)].reshape((rows + 2) * LANES, wide)
                work[p] = jnp.dot(w1[...], piece, preferred_element_type=jnp.float32)
                return carry

            lax.fori_loop(0, planes + 4, first, 0)

            def hidden(p, carry):
                summed = (
                    work[p, 0:size] + work[p + 1, size : 2 * size]
                    + work[p + 2, 2 * size : 3 * size] + bias[0]
                )
                summed = jnp.maximum(summed, 0.0)
                at = d * planes + p - 1
                for j in range(rows):
                    row = q * rows + base + j - 1
                    ok = (at >= 0) & (at < depth_n * planes) & (row >= 0) & (row < rows_n * rows)
                    part = summed[j * regs : (j + 1) * regs]
                    part = jnp.where(inside & ok, part, 0.0)
                    part = part.astype(jnp.bfloat16).astype(jnp.float32)
                    lines = [pltpu.roll(part, 1, 1), part, pltpu.roll(part, wide - 1, 1)]
                    lines.append(jnp.zeros((LANES - 3 * regs, wide), jnp.float32))
                    hid[b, p, base + j] = jnp.concatenate(lines, axis=0).astype(jnp.bfloat16)
                return carry

            lax.fori_loop(0, planes + 2, hidden, 0)

        def second(p, carry):
            piece = hid[b, p].reshape((rows + 2) * LANES, wide)
            work[p] = jnp.dot(w2[...], piece, preferred_element_type=jnp.float32)
            return carry

        lax.fori_loop(0, planes + 2, second, 0)

        def finish(p, carry):
            summed = (
                work[p, 0:size] + work[p + 1, size : 2 * size]
                + work[p + 2, 2 * size : 3 * size] + bias[1]
            )
            for j in range(rows):
                out_ref[b, p, j] = summed[j * regs : (j + 1) * regs, 0:columns].astype(jnp.bfloat16)
            return carry

        lax.fori_loop(0, planes, finish, 0)

    for (dd, dq), copy in every:
        @pl.when(exists(dd, dq))
        def _():
            copy.wait_send()


def body(
    depth_n, rows_n, ref_feat, src_feat, block_index, blend, conv_first, bias_first, conv_second, bias_second
):
    scenes, views, rows, flat = src_feat.shape
    planes, columns = blend.shape[2], blend.shape[4]
    channels, regs = conv_first.shape[4], conv_first.shape[3]
    feats = flat // columns
    groups = channels - feats
    per_group = feats // groups
    tail = columns - LANES
    packed = feats + groups

    cube = jnp.concatenate([src_feat, ref_feat[:, None]], axis=1)
    cube = cube.reshape(scenes, views + 1, rows, groups, per_group, columns)
    main = jnp.moveaxis(cube[..., :LANES], 4, 3).reshape(scenes, views + 1, rows, feats, LANES)
    ends = cube[..., LANES:].reshape(scenes, views + 1, rows, groups, per_group * tail)
    feat_in = jnp.moveaxis(jnp.concatenate([main, ends], axis=3), 1, 0)

    below = (block_index < lax.axis_index("rows"))[:, :, :, :, None]
    lower = jnp.where(below, blend, jnp.zeros_like(blend))
    upper = jnp.where(below, jnp.ones_like(blend), blend)
    coef = jnp.concatenate([lower, upper], axis=1)
    coef = jnp.concatenate([coef[..., :LANES]] + [coef[..., LANES:]] * per_group, axis=4)
    coef_in = jnp.transpose(coef, (2, 0, 3, 1, 4))

    wide = 2 * LANES
    dims = (scenes, views, rows, planes, feats, groups, columns, regs, depth_n, rows_n)
    bf16, f32 = jnp.bfloat16, jnp.float32
    out = pl.pallas_call(
        functools.partial(kernel, dims),
        out_shape=jax.ShapeDtypeStruct((scenes, planes, rows, regs, columns), bf16),
        in_specs=[pl.BlockSpec(memory_space=pltpu.VMEM)] * 6,
        out_specs=pl.BlockSpec(memory_space=pltpu.VMEM),
        scratch_shapes=[
            pltpu.VMEM((5, views + 1, scenes, rows, packed, LANES), bf16),
            pltpu.VMEM((3, planes + 4, scenes, rows, 2 * views, wide), bf16),
            pltpu.VMEM((scenes, planes + 4, 3 * rows, LANES, wide), bf16),
            pltpu.VMEM((scenes, planes + 2, rows + 2, LANES, wide), bf16),
            pltpu.VMEM((planes + 4, 3 * rows * regs, wide), f32),
            pltpu.VMEM((3 * rows * regs, (rows + 2) * LANES), bf16),
            pltpu.VMEM((3 * rows * regs, (rows + 2) * LANES), bf16),
            pltpu.VMEM((3 * views + 1, packed, LANES), f32),
            pltpu.VMEM((2, rows * regs, wide), f32),
            pltpu.SemaphoreType.DMA((12,)),
            pltpu.SemaphoreType.DMA((12,)),
            pltpu.SemaphoreType.DMA((2,)),
        ],
        compiler_params=pltpu.CompilerParams(
            collective_id=0, has_side_effects=True, vmem_limit_bytes=56 << 20
        ),
    )(feat_in, coef_in, conv_first, bias_first[None], conv_second, bias_second[None])
    return out.reshape(scenes, planes, rows, regs * columns)


def solution(mesh):
    in_specs = (
        P(None, "rows", None),
        P(None, None, "rows", None),
        P(None, None, "depth", "rows"),
        P(None, None, "depth", "rows", None),
        P(),
        P(),
        P(),
        P(),
    )
    out_specs = P(None, "depth", "rows", None)
    step = functools.partial(body, mesh.shape["depth"], mesh.shape["rows"])
    return jax.shard_map(step, mesh=mesh, in_specs=in_specs, out_specs=out_specs, check_vma=False)
```

```python
import functools

import jax
import jax.numpy as jnp
from jax import lax
from jax.experimental import pallas as pl
from jax.experimental.pallas import tpu as pltpu
from jax.sharding import PartitionSpec as P

MESH = pl.DeviceIdType.MESH
LANES = 128
NEAR = ((0, 1), (0, -1), (1, 0), (-1, 0), (1, 1), (1, -1), (-1, 1), (-1, -1))
FAR = ((0, 2), (0, -2))


def run(count, step, most=5):
    unroll = max(k for k in range(1, most + 1) if count % k == 0)
    lax.fori_loop(0, count, step, 0, unroll=unroll)


def kernel(
    dims, feat_in, coef_in, k1_in, b1_in, k2_in, b2_in, out_ref,
    feat, coef, vol, hid, work, w1, w2, prep, bias, send_sem, recv_sem, local_sem,
):
    scenes, views, rows, planes, feats, groups, columns, regs, depth_n, rows_n = dims
    channels = groups + feats
    per_group = feats // groups
    packed = feat_in.shape[3]
    half = scenes // 2
    wide = 2 * LANES
    tail = columns - LANES
    d = lax.axis_index("depth")
    q = lax.axis_index("rows")
    side = lax.rem(d, 2)
    mate = d + 1 - 2 * side

    def exists(dd, dq):
        return (d + dd >= 0) & (d + dd < depth_n) & (q + dq >= 0) & (q + dq < rows_n)

    barrier = pltpu.get_barrier_semaphore()
    for dd, dq in NEAR + FAR:
        @pl.when(exists(dd, dq))
        def _():
            pl.semaphore_signal(barrier, inc=1, device_id=(d + dd, q + dq), device_id_type=MESH)

    local = [
        pltpu.make_async_copy(feat_in, feat.at[2], local_sem.at[0]),
        pltpu.make_async_copy(coef_in, coef.at[1, pl.ds(2, planes)], local_sem.at[1]),
    ]
    for copy in local:
        copy.start()

    def feat_copy(dq, k):
        slot = 2 - dq
        count = views + 1 if abs(dq) == 1 else views
        return pltpu.make_async_remote_copy(
            src_ref=feat_in.at[pl.ds(side * half, half), pl.ds(0, count)],
            dst_ref=feat.at[slot, pl.ds(side * half, half), pl.ds(0, count)],
            send_sem=send_sem.at[k], recv_sem=recv_sem.at[k],
            device_id=(d, q + dq), device_id_type=MESH,
        )

    def mate_copy(dq, k):
        slot = 2 - dq
        count = views + 1 if abs(dq) == 1 else views
        part = feat.at[slot, pl.ds(side * half, half), pl.ds(0, count)]
        return pltpu.make_async_remote_copy(
            src_ref=part, dst_ref=part,
            send_sem=send_sem.at[k], recv_sem=recv_sem.at[k],
            device_id=(mate, q), device_id_type=MESH,
        )

    def coef_copy(dd, dq, k):
        if dd == 0:
            first, count, at = 0, planes, 2
        elif dd == 1:
            first, count, at = planes - 2, 2, 0
        else:
            first, count, at = 0, 2, planes + 2
        return pltpu.make_async_remote_copy(
            src_ref=coef_in.at[pl.ds(first, count)],
            dst_ref=coef.at[1 - dq, pl.ds(at, count)],
            send_sem=send_sem.at[k], recv_sem=recv_sem.at[k],
            device_id=(d + dd, q + dq), device_id_type=MESH,
        )

    near_feat = [((0, dq), feat_copy(dq, i)) for i, dq in enumerate((1, -1))]
    far_feat = [((0, dq), feat_copy(dq, 2 + i)) for i, dq in enumerate((2, -2))]
    depth_coef = [((dd, 0), coef_copy(dd, 0, 4 + i)) for i, dd in enumerate((1, -1))]
    side_coef = [
        ((dd, dq), coef_copy(dd, dq, 6 + i))
        for i, (dd, dq) in enumerate([m for m in NEAR if m[1] != 0])
    ]
    every = near_feat + depth_coef + side_coef + far_feat
    near_mate = [((0, dq), mate_copy(dq, 12 + i)) for i, dq in enumerate((1, -1))]
    far_mate = [((0, dq), mate_copy(dq, 14 + i)) for i, dq in enumerate((2, -2))]

    for slot, gone in ((0, q < 2), (1, q < 1), (3, q + 1 >= rows_n), (4, q + 2 >= rows_n)):
        @pl.when(gone)
        def _():
            feat[slot] = jnp.zeros(feat.shape[1:], feat.dtype)

    beside = 1 + lax.div(d + depth_n - 1, depth_n) + lax.div(2 * depth_n - 2 - d, depth_n)
    above = 1 + lax.div(q + rows_n - 1, rows_n) + lax.div(2 * rows_n - 2 - q, rows_n)
    beyond = lax.div(q + rows_n - 2, rows_n) + lax.div(2 * rows_n - 3 - q, rows_n)
    pl.semaphore_wait(barrier, beside * above - 1 + beyond)

    for (dd, dq), copy in every:
        @pl.when(exists(dd, dq))
        def _():
            copy.start()

    def arrive(pairs):
        for (dd, dq), copy in pairs:
            @pl.when(exists(-dd, -dq))
            def _():
                copy.wait_recv()

    def hand_on(pairs):
        for (dd, dq), copy in pairs:
            @pl.when(exists(-dd, -dq))
            def _():
                copy.start()

    def place(kernel_in, count, span, target, dest):
        for a in range(3):
            for r in range(3):
                line = jnp.zeros((regs, span), jnp.float32)
                for s in range(3):
                    c = lax.broadcasted_iota(jnp.int32, (count, span), 0)
                    k = lax.broadcasted_iota(jnp.int32, (count, span), 1)
                    pick = jnp.where(dest(s, c) == k, 1.0, 0.0).astype(jnp.bfloat16)
                    line = line + jnp.dot(kernel_in[a, r, s], pick, preferred_element_type=jnp.float32)
                line = line.astype(jnp.bfloat16)
                for j in range(rows):
                    target[pl.ds((a * rows + j) * regs, regs), pl.ds((j + r) * span, span)] = line

    def first_dest(s, c):
        f = c - groups
        spread_at = s * feats + (f % per_group) * groups + f // per_group
        return jnp.where(c < groups, 3 * feats + s * groups + c, spread_at)

    w1[...] = jnp.zeros(w1.shape, w1.dtype)
    w2[...] = jnp.zeros(w2.shape, w2.dtype)
    place(k1_in, channels, LANES, w1, first_dest)
    place(k2_in, regs, LANES, w2, lambda s, c: s * regs + c)
    eye = lax.broadcasted_iota(jnp.int32, (regs, regs), 0) == lax.broadcasted_iota(
        jnp.int32, (regs, regs), 1
    )
    for i, b_in in enumerate((b1_in, b2_in)):
        column = jnp.sum(jnp.where(eye, b_in[...], 0.0), axis=1, keepdims=True)
        bias[i] = jnp.broadcast_to(jnp.concatenate([column] * rows, axis=0), (rows * regs, wide))

    for copy in local:
        copy.wait()

    lane = lax.broadcasted_iota(jnp.int32, (groups, LANES), 1)
    in_tail = lane < tail

    def unpack(tail_packed):
        parts = []
        for j in range(per_group):
            part = tail_packed if j == 0 else pltpu.roll(tail_packed, LANES - tail * j, 1)
            parts.append(jnp.where(in_tail, part, 0.0))
        return parts

    def volume_rows(block):
        for b in range(scenes):
            for m in range(rows):
                ref = feat[block + 1, b, views, m].astype(jnp.float32)
                prep[3 * views] = ref
                for v in range(views):
                    low = feat[block, b, v, m].astype(jnp.float32)
                    mid = feat[block + 1, b, v, m].astype(jnp.float32)
                    up = feat[block + 2, b, v, m].astype(jnp.float32)
                    prep[v] = mid - ref
                    prep[views + v] = low - mid
                    prep[2 * views + v] = up - mid
                row = (block - 1) * rows + m
                row_ok = (q * rows + row >= 0) & (q * rows + row < rows_n * rows)

                def plane(p, carry):
                    at = d * planes + p - 2
                    ok = row_ok & (at >= 0) & (at < depth_n * planes)
                    weights = coef[block, p, b, m].astype(jnp.float32)
                    others = 1.0 - weights
                    total = None
                    for v in range(views):
                        cl = weights[v : v + 1]
                        cu = others[views + v : views + v + 1]
                        both = []
                        for lo, hi, l0 in ((0, feats, 0), (feats, packed, LANES)):
                            both.append(
                                prep[v, lo:hi]
                                + cl[:, l0 : l0 + LANES] * prep[views + v, lo:hi]
                                + cu[:, l0 : l0 + LANES] * prep[2 * views + v, lo:hi]
                            )
                        if total is None:
                            total = both
                            square = [u * u for u in both]
                        else:
                            total = [t + u for t, u in zip(total, both)]
                            square = [t + u * u for t, u in zip(square, both)]
                    share = 1.0 / (views + 1.0)
                    spread = [(s2 - t * t * share) * share for s2, t in zip(square, total)]
                    refs = [prep[3 * views, 0:feats], prep[3 * views, feats:packed]]
                    product = [r * (t + (1.0 * views) * r) for r, t in zip(refs, total)]
                    scale = 1.0 / (views * per_group)
                    head = product[0][0:groups]
                    for j in range(1, per_group):
                        head = head + product[0][j * groups : (j + 1) * groups]
                    rest = product[1]
                    step = LANES // 2
                    while step >= tail:
                        rest = rest + pltpu.roll(rest, step, 1)
                        step //= 2
                    corr = jnp.concatenate([head, jnp.where(in_tail, rest, 0.0)], axis=1) * scale
                    ends = unpack(spread[1])
                    full = jnp.concatenate(
                        [jnp.concatenate([spread[0], jnp.concatenate(ends, axis=0)], axis=1), corr],
                        axis=0,
                    )
                    full = jnp.where(ok, full, 0.0)
                    left = pltpu.roll(full, 1, 1)
                    right = pltpu.roll(full, wide - 1, 1)
                    lines = [left[:feats], full[:feats], right[:feats]]
                    lines += [left[feats:], full[feats:], right[feats:]]
                    lines.append(jnp.zeros((LANES - 3 * channels, wide), jnp.float32))
                    vol[b, p, row + rows] = jnp.concatenate(lines, axis=0).astype(jnp.bfloat16)
                    return carry

                run(planes + 4, plane)

    arrive(near_feat)
    hand_on(near_mate)
    arrive(depth_coef)
    arrive(near_mate)
    volume_rows(1)
    arrive(far_feat)
    hand_on(far_mate)
    arrive(side_coef)
    arrive(far_mate)
    volume_rows(0)
    volume_rows(2)

    size = rows * regs
    inside = lax.broadcasted_iota(jnp.int32, (regs, wide), 1) < columns
    for b in range(scenes):
        for pair in range(2):
            base = pair * rows

            def first(p, carry):
                piece = vol[b, p, pl.ds(base, rows + 2)].reshape((rows + 2) * LANES, wide)
                work[p] = jnp.dot(w1[...], piece, preferred_element_type=jnp.float32)
                return carry

            run(planes + 4, first)

            def hidden(p, carry):
                summed = (
                    work[p, 0:size] + work[p + 1, size : 2 * size]
                    + work[p + 2, 2 * size : 3 * size] + bias[0]
                )
                summed = jnp.maximum(summed, 0.0)
                at = d * planes + p - 1
                for j in range(rows):
                    row = q * rows + base + j - 1
                    ok = (at >= 0) & (at < depth_n * planes) & (row >= 0) & (row < rows_n * rows)
                    part = summed[j * regs : (j + 1) * regs]
                    part = jnp.where(inside & ok, part, 0.0)
                    part = part.astype(jnp.bfloat16).astype(jnp.float32)
                    lines = [pltpu.roll(part, 1, 1), part, pltpu.roll(part, wide - 1, 1)]
                    lines.append(jnp.zeros((LANES - 3 * regs, wide), jnp.float32))
                    hid[b, p, base + j] = jnp.concatenate(lines, axis=0).astype(jnp.bfloat16)
                return carry

            run(planes + 2, hidden)

        def second(p, carry):
            piece = hid[b, p].reshape((rows + 2) * LANES, wide)
            work[p] = jnp.dot(w2[...], piece, preferred_element_type=jnp.float32)
            return carry

        run(planes + 2, second)

        def finish(p, carry):
            summed = (
                work[p, 0:size] + work[p + 1, size : 2 * size]
                + work[p + 2, 2 * size : 3 * size] + bias[1]
            )
            for j in range(rows):
                out_ref[b, p, j] = summed[j * regs : (j + 1) * regs, 0:columns].astype(jnp.bfloat16)
            return carry

        run(planes, finish)

    for (dd, dq), copy in every:
        @pl.when(exists(dd, dq))
        def _():
            copy.wait_send()

    for (dd, dq), copy in near_mate + far_mate:
        @pl.when(exists(-dd, -dq))
        def _():
            copy.wait_send()


def body(
    depth_n, rows_n, ref_feat, src_feat, block_index, blend, conv_first, bias_first, conv_second, bias_second
):
    scenes, views, rows, flat = src_feat.shape
    planes, columns = blend.shape[2], blend.shape[4]
    channels, regs = conv_first.shape[4], conv_first.shape[3]
    feats = flat // columns
    groups = channels - feats
    per_group = feats // groups
    tail = columns - LANES
    packed = feats + groups

    cube = jnp.concatenate([src_feat, ref_feat[:, None]], axis=1)
    cube = cube.reshape(scenes, views + 1, rows, groups, per_group, columns)
    main = jnp.moveaxis(cube[..., :LANES], 4, 3).reshape(scenes, views + 1, rows, feats, LANES)
    ends = cube[..., LANES:].reshape(scenes, views + 1, rows, groups, per_group * tail)
    feat_in = jnp.concatenate([main, ends], axis=3)

    below = (block_index < lax.axis_index("rows"))[:, :, :, :, None]
    lower = jnp.where(below, blend, jnp.zeros_like(blend))
    upper = jnp.where(below, jnp.ones_like(blend), blend)
    coef = jnp.concatenate([lower, upper], axis=1)
    coef = jnp.concatenate([coef[..., :LANES]] + [coef[..., LANES:]] * per_group, axis=4)
    coef_in = jnp.transpose(coef, (2, 0, 3, 1, 4))

    wide = 2 * LANES
    dims = (scenes, views, rows, planes, feats, groups, columns, regs, depth_n, rows_n)
    bf16, f32 = jnp.bfloat16, jnp.float32
    out = pl.pallas_call(
        functools.partial(kernel, dims),
        out_shape=jax.ShapeDtypeStruct((scenes, planes, rows, regs, columns), bf16),
        in_specs=[pl.BlockSpec(memory_space=pltpu.VMEM)] * 6,
        out_specs=pl.BlockSpec(memory_space=pltpu.VMEM),
        scratch_shapes=[
            pltpu.VMEM((5, scenes, views + 1, rows, packed, LANES), bf16),
            pltpu.VMEM((3, planes + 4, scenes, rows, 2 * views, wide), bf16),
            pltpu.VMEM((scenes, planes + 4, 3 * rows, LANES, wide), bf16),
            pltpu.VMEM((scenes, planes + 2, rows + 2, LANES, wide), bf16),
            pltpu.VMEM((planes + 4, 3 * rows * regs, wide), f32),
            pltpu.VMEM((3 * rows * regs, (rows + 2) * LANES), bf16),
            pltpu.VMEM((3 * rows * regs, (rows + 2) * LANES), bf16),
            pltpu.VMEM((3 * views + 1, packed, LANES), f32),
            pltpu.VMEM((2, rows * regs, wide), f32),
            pltpu.SemaphoreType.DMA((16,)),
            pltpu.SemaphoreType.DMA((16,)),
            pltpu.SemaphoreType.DMA((2,)),
        ],
        compiler_params=pltpu.CompilerParams(
            collective_id=0, has_side_effects=True, vmem_limit_bytes=56 << 20
        ),
    )(feat_in, coef_in, conv_first, bias_first[None], conv_second, bias_second[None])
    return out.reshape(scenes, planes, rows, regs * columns)


def solution(mesh):
    in_specs = (
        P(None, "rows", None),
        P(None, None, "rows", None),
        P(None, None, "depth", "rows"),
        P(None, None, "depth", "rows", None),
        P(),
        P(),
        P(),
        P(),
    )
    out_specs = P(None, "depth", "rows", None)
    step = functools.partial(body, mesh.shape["depth"], mesh.shape["rows"])
    return jax.shard_map(step, mesh=mesh, in_specs=in_specs, out_specs=out_specs, check_vma=False)
```

```python
import functools

import jax
import jax.numpy as jnp
from jax import lax
from jax.experimental import pallas as pl
from jax.experimental.pallas import tpu as pltpu
from jax.sharding import PartitionSpec as P

MESH = pl.DeviceIdType.MESH
LANES = 128
NEAR = ((0, 1), (0, -1), (1, 0), (-1, 0), (1, 1), (1, -1), (-1, 1), (-1, -1))
FAR = ((0, 2), (0, -2))


def run(count, step, most=5):
    unroll = max(k for k in range(1, most + 1) if count % k == 0)
    lax.fori_loop(0, count, step, 0, unroll=unroll)


def kernel(
    dims, feat_in, coef_in, k1_in, b1_in, k2_in, b2_in, out_ref,
    feat, coef, vol, hid, work, w1, w2, prep, bias, send_sem, recv_sem, local_sem,
):
    scenes, views, rows, planes, feats, groups, columns, regs, depth_n, rows_n = dims
    channels = groups + feats
    per_group = feats // groups
    packed = feat_in.shape[3]
    half = scenes // 2
    wide = 2 * LANES
    tail = columns - LANES
    d = lax.axis_index("depth")
    q = lax.axis_index("rows")
    side = lax.rem(d, 2)
    mate = d + 1 - 2 * side

    def exists(dd, dq):
        return (d + dd >= 0) & (d + dd < depth_n) & (q + dq >= 0) & (q + dq < rows_n)

    barrier = pltpu.get_barrier_semaphore()
    for dd, dq in NEAR + FAR:
        @pl.when(exists(dd, dq))
        def _():
            pl.semaphore_signal(barrier, inc=1, device_id=(d + dd, q + dq), device_id_type=MESH)

    local = [
        pltpu.make_async_copy(feat_in, feat.at[2], local_sem.at[0]),
        pltpu.make_async_copy(coef_in, coef.at[1, pl.ds(2, planes)], local_sem.at[1]),
    ]
    for copy in local:
        copy.start()

    def feat_copy(dq, k):
        slot = 2 - dq
        count = views + 1 if abs(dq) == 1 else views
        return pltpu.make_async_remote_copy(
            src_ref=feat_in.at[pl.ds(side * half, half), pl.ds(0, count)],
            dst_ref=feat.at[slot, pl.ds(side * half, half), pl.ds(0, count)],
            send_sem=send_sem.at[k], recv_sem=recv_sem.at[k],
            device_id=(d, q + dq), device_id_type=MESH,
        )

    def mate_copy(dq, k):
        slot = 2 - dq
        count = views + 1 if abs(dq) == 1 else views
        part = feat.at[slot, pl.ds(side * half, half), pl.ds(0, count)]
        return pltpu.make_async_remote_copy(
            src_ref=part, dst_ref=part,
            send_sem=send_sem.at[k], recv_sem=recv_sem.at[k],
            device_id=(mate, q), device_id_type=MESH,
        )

    def coef_copy(dd, dq, k):
        if dd == 0:
            first, count, at = 0, planes, 2
        elif dd == 1:
            first, count, at = planes - 2, 2, 0
        else:
            first, count, at = 0, 2, planes + 2
        return pltpu.make_async_remote_copy(
            src_ref=coef_in.at[pl.ds(first, count)],
            dst_ref=coef.at[1 - dq, pl.ds(at, count)],
            send_sem=send_sem.at[k], recv_sem=recv_sem.at[k],
            device_id=(d + dd, q + dq), device_id_type=MESH,
        )

    near_feat = [((0, dq), feat_copy(dq, i)) for i, dq in enumerate((1, -1))]
    far_feat = [((0, dq), feat_copy(dq, 2 + i)) for i, dq in enumerate((2, -2))]
    depth_coef = [((dd, 0), coef_copy(dd, 0, 4 + i)) for i, dd in enumerate((1, -1))]
    side_coef = [
        ((dd, dq), coef_copy(dd, dq, 6 + i))
        for i, (dd, dq) in enumerate([m for m in NEAR if m[1] != 0])
    ]
    every = near_feat + depth_coef + far_feat + side_coef
    near_mate = [((0, dq), mate_copy(dq, 12 + i)) for i, dq in enumerate((1, -1))]
    far_mate = [((0, dq), mate_copy(dq, 14 + i)) for i, dq in enumerate((2, -2))]

    for slot, gone in ((0, q < 2), (1, q < 1), (3, q + 1 >= rows_n), (4, q + 2 >= rows_n)):
        @pl.when(gone)
        def _():
            feat[slot] = jnp.zeros(feat.shape[1:], feat.dtype)

    beside = 1 + lax.div(d + depth_n - 1, depth_n) + lax.div(2 * depth_n - 2 - d, depth_n)
    above = 1 + lax.div(q + rows_n - 1, rows_n) + lax.div(2 * rows_n - 2 - q, rows_n)
    beyond = lax.div(q + rows_n - 2, rows_n) + lax.div(2 * rows_n - 3 - q, rows_n)
    pl.semaphore_wait(barrier, beside * above - 1 + beyond)

    for (dd, dq), copy in every:
        @pl.when(exists(dd, dq))
        def _():
            copy.start()

    def arrive(pairs):
        for (dd, dq), copy in pairs:
            @pl.when(exists(-dd, -dq))
            def _():
                copy.wait_recv()

    def hand_on(pairs):
        for (dd, dq), copy in pairs:
            @pl.when(exists(-dd, -dq))
            def _():
                copy.start()

    def place(kernel_in, count, span, target, dest, order=None):
        for a in range(3):
            for r in range(3):
                line = jnp.zeros((regs, span), jnp.float32)
                for s in range(3):
                    c = lax.broadcasted_iota(jnp.int32, (count, span), 0)
                    k = lax.broadcasted_iota(jnp.int32, (count, span), 1)
                    pick = jnp.where(dest(s, c) == k, 1.0, 0.0).astype(jnp.bfloat16)
                    line = line + jnp.dot(kernel_in[a, r, s], pick, preferred_element_type=jnp.float32)
                line = line.astype(jnp.bfloat16)
                if order is not None:
                    line = jnp.dot(order, line, preferred_element_type=jnp.float32)
                    line = line.astype(jnp.bfloat16)
                for j in range(rows):
                    target[pl.ds((a * rows + j) * regs, regs), pl.ds((j + r) * span, span)] = line

    def first_dest(s, c):
        f = c - groups
        spread_at = s * feats + (f % per_group) * groups + f // per_group
        return jnp.where(c < groups, 3 * feats + s * groups + c, spread_at)

    w1[...] = jnp.zeros(w1.shape, w1.dtype)
    w2[...] = jnp.zeros(w2.shape, w2.dtype)
    place(k1_in, channels, LANES, w1, first_dest)
    per_out = regs // groups
    at_row = lax.broadcasted_iota(jnp.int32, (regs, regs), 0)
    at_channel = lax.broadcasted_iota(jnp.int32, (regs, regs), 1)
    order = at_channel == (at_row % groups) * per_out + at_row // groups
    place(
        k2_in, regs, LANES, w2, lambda s, c: s * regs + c,
        jnp.where(order, 1.0, 0.0).astype(jnp.bfloat16),
    )
    for i, (b_in, mask) in enumerate(((b1_in, at_row == at_channel), (b2_in, order))):
        column = jnp.sum(jnp.where(mask, b_in[...], 0.0), axis=1, keepdims=True)
        bias[i] = jnp.broadcast_to(jnp.concatenate([column] * rows, axis=0), (rows * regs, wide))

    for copy in local:
        copy.wait()

    lane = lax.broadcasted_iota(jnp.int32, (groups, LANES), 1)
    in_tail = lane < tail

    def unpack(tail_packed):
        parts = []
        for j in range(per_group):
            part = tail_packed if j == 0 else pltpu.roll(tail_packed, LANES - tail * j, 1)
            parts.append(jnp.where(in_tail, part, 0.0))
        return parts

    def volume_rows(block):
        for b in range(scenes):
            for m in range(rows):
                ref = feat[block + 1, b, views, m].astype(jnp.float32)
                prep[3 * views] = ref
                for v in range(views):
                    low = feat[block, b, v, m].astype(jnp.float32)
                    mid = feat[block + 1, b, v, m].astype(jnp.float32)
                    up = feat[block + 2, b, v, m].astype(jnp.float32)
                    prep[v] = mid - ref
                    prep[views + v] = low - mid
                    prep[2 * views + v] = up - mid
                row = (block - 1) * rows + m
                row_ok = (q * rows + row >= 0) & (q * rows + row < rows_n * rows)

                def plane(p, carry):
                    at = d * planes + p - 2
                    ok = row_ok & (at >= 0) & (at < depth_n * planes)
                    weights = coef[block, p, b, m].astype(jnp.float32)
                    others = 1.0 - weights
                    total = None
                    for v in range(views):
                        cl = weights[v : v + 1]
                        cu = others[views + v : views + v + 1]
                        both = []
                        for lo, hi, l0 in ((0, feats, 0), (feats, packed, LANES)):
                            both.append(
                                prep[v, lo:hi]
                                + cl[:, l0 : l0 + LANES] * prep[views + v, lo:hi]
                                + cu[:, l0 : l0 + LANES] * prep[2 * views + v, lo:hi]
                            )
                        if total is None:
                            total = both
                            square = [u * u for u in both]
                        else:
                            total = [t + u for t, u in zip(total, both)]
                            square = [t + u * u for t, u in zip(square, both)]
                    share = 1.0 / (views + 1.0)
                    spread = [(s2 - t * t * share) * share for s2, t in zip(square, total)]
                    refs = [prep[3 * views, 0:feats], prep[3 * views, feats:packed]]
                    product = [r * (t + (1.0 * views) * r) for r, t in zip(refs, total)]
                    scale = 1.0 / (views * per_group)
                    head = product[0][0:groups]
                    for j in range(1, per_group):
                        head = head + product[0][j * groups : (j + 1) * groups]
                    rest = product[1]
                    step = LANES // 2
                    while step >= tail:
                        rest = rest + pltpu.roll(rest, step, 1)
                        step //= 2
                    corr = jnp.concatenate([head, jnp.where(in_tail, rest, 0.0)], axis=1) * scale
                    ends = unpack(spread[1])
                    full = jnp.concatenate(
                        [jnp.concatenate([spread[0], jnp.concatenate(ends, axis=0)], axis=1), corr],
                        axis=0,
                    )
                    full = jnp.where(ok, full, 0.0)
                    left = pltpu.roll(full, 1, 1)
                    right = pltpu.roll(full, wide - 1, 1)
                    lines = [left[:feats], full[:feats], right[:feats]]
                    lines += [left[feats:], full[feats:], right[feats:]]
                    lines.append(jnp.zeros((LANES - 3 * channels, wide), jnp.float32))
                    vol[b, p, row + rows] = jnp.concatenate(lines, axis=0).astype(jnp.bfloat16)
                    return carry

                run(planes + 4, plane)

    arrive(near_feat)
    hand_on(near_mate)
    arrive(depth_coef)
    arrive(near_mate)
    volume_rows(1)
    arrive(far_feat)
    hand_on(far_mate)

    size = rows * regs

    def products(own):
        for b in range(scenes):
            for pair in range(2):
                start = rows if own else 2 * rows * pair
                line = w1.at[:, pl.ds((start - pair * rows) * LANES, rows * LANES)]

                def first(p, carry):
                    piece = vol[b, p, pl.ds(start, rows)].reshape(rows * LANES, wide)
                    value = jnp.dot(line[...], piece, preferred_element_type=jnp.float32)
                    if not own:
                        value = value + work[2 * b + pair, p]
                    work[2 * b + pair, p] = value
                    return carry

                run(planes + 4, first)

    products(True)
    arrive(side_coef)
    arrive(far_mate)
    volume_rows(0)
    volume_rows(2)
    products(False)
    inside = lax.broadcasted_iota(jnp.int32, (regs, wide), 1) < columns
    for b in range(scenes):
        for pair in range(2):
            base = pair * rows
            at_work = work.at[2 * b + pair]

            def hidden(p, carry):
                summed = (
                    at_work[p, 0:size] + at_work[p + 1, size : 2 * size]
                    + at_work[p + 2, 2 * size : 3 * size] + bias[0]
                )
                summed = jnp.maximum(summed, 0.0)
                at = d * planes + p - 1
                for j in range(rows):
                    row = q * rows + base + j - 1
                    ok = (at >= 0) & (at < depth_n * planes) & (row >= 0) & (row < rows_n * rows)
                    part = summed[j * regs : (j + 1) * regs]
                    part = jnp.where(inside & ok, part, 0.0)
                    part = part.astype(jnp.bfloat16).astype(jnp.float32)
                    lines = [pltpu.roll(part, 1, 1), part, pltpu.roll(part, wide - 1, 1)]
                    lines.append(jnp.zeros((LANES - 3 * regs, wide), jnp.float32))
                    hid[b, p, base + j] = jnp.concatenate(lines, axis=0).astype(jnp.bfloat16)
                return carry

            run(planes + 2, hidden)

        def second(p, carry):
            piece = hid[b, p].reshape((rows + 2) * LANES, wide)
            work[0, p] = jnp.dot(w2[...], piece, preferred_element_type=jnp.float32)
            return carry

        run(planes + 2, second)

        def finish(p, carry):
            summed = (
                work[0, p, 0:size] + work[0, p + 1, size : 2 * size]
                + work[0, p + 2, 2 * size : 3 * size] + bias[1]
            )
            for j in range(rows):
                for t in range(per_out):
                    first_row = j * regs + t * groups
                    part = summed[first_row : first_row + groups, 0:columns]
                    out_ref[b, p, j, :, pl.ds(t * columns, columns)] = part.astype(jnp.bfloat16)
            return carry

        run(planes, finish)

    for (dd, dq), copy in every:
        @pl.when(exists(dd, dq))
        def _():
            copy.wait_send()

    for (dd, dq), copy in near_mate + far_mate:
        @pl.when(exists(-dd, -dq))
        def _():
            copy.wait_send()


def body(
    depth_n, rows_n, ref_feat, src_feat, block_index, blend, conv_first, bias_first, conv_second, bias_second
):
    scenes, views, rows, flat = src_feat.shape
    planes, columns = blend.shape[2], blend.shape[4]
    channels, regs = conv_first.shape[4], conv_first.shape[3]
    feats = flat // columns
    groups = channels - feats
    per_group = feats // groups
    tail = columns - LANES
    packed = feats + groups

    cube = jnp.concatenate([src_feat, ref_feat[:, None]], axis=1)
    cube = cube.reshape(scenes, views + 1, rows, groups, per_group, columns)
    main = jnp.moveaxis(cube[..., :LANES], 4, 3).reshape(scenes, views + 1, rows, feats, LANES)
    ends = cube[..., LANES:].reshape(scenes, views + 1, rows, groups, per_group * tail)
    feat_in = jnp.concatenate([main, ends], axis=3)

    below = (block_index < lax.axis_index("rows"))[:, :, :, :, None]
    lower = jnp.where(below, blend, jnp.zeros_like(blend))
    upper = jnp.where(below, jnp.ones_like(blend), blend)
    coef = jnp.concatenate([lower, upper], axis=1)
    coef = jnp.concatenate([coef[..., :LANES]] + [coef[..., LANES:]] * per_group, axis=4)
    coef_in = jnp.transpose(coef, (2, 0, 3, 1, 4))

    wide = 2 * LANES
    dims = (scenes, views, rows, planes, feats, groups, columns, regs, depth_n, rows_n)
    bf16, f32 = jnp.bfloat16, jnp.float32
    out = pl.pallas_call(
        functools.partial(kernel, dims),
        out_shape=jax.ShapeDtypeStruct((scenes, planes, rows, groups, regs // groups * columns), bf16),
        in_specs=[pl.BlockSpec(memory_space=pltpu.VMEM)] * 6,
        out_specs=pl.BlockSpec(memory_space=pltpu.VMEM),
        scratch_shapes=[
            pltpu.VMEM((5, scenes, views + 1, rows, packed, LANES), bf16),
            pltpu.VMEM((3, planes + 4, scenes, rows, 2 * views, wide), bf16),
            pltpu.VMEM((scenes, planes + 4, 3 * rows, LANES, wide), bf16),
            pltpu.VMEM((scenes, planes + 2, rows + 2, LANES, wide), bf16),
            pltpu.VMEM((2 * scenes, planes + 4, 3 * rows * regs, wide), f32),
            pltpu.VMEM((3 * rows * regs, (rows + 2) * LANES), bf16),
            pltpu.VMEM((3 * rows * regs, (rows + 2) * LANES), bf16),
            pltpu.VMEM((3 * views + 1, packed, LANES), f32),
            pltpu.VMEM((2, rows * regs, wide), f32),
            pltpu.SemaphoreType.DMA((16,)),
            pltpu.SemaphoreType.DMA((16,)),
            pltpu.SemaphoreType.DMA((2,)),
        ],
        compiler_params=pltpu.CompilerParams(
            collective_id=0, has_side_effects=True, vmem_limit_bytes=56 << 20
        ),
    )(feat_in, coef_in, conv_first, bias_first[None], conv_second, bias_second[None])
    return out.reshape(scenes, planes, rows, regs * columns)


def solution(mesh):
    in_specs = (
        P(None, "rows", None),
        P(None, None, "rows", None),
        P(None, None, "depth", "rows"),
        P(None, None, "depth", "rows", None),
        P(),
        P(),
        P(),
        P(),
    )
    out_specs = P(None, "depth", "rows", None)
    step = functools.partial(body, mesh.shape["depth"], mesh.shape["rows"])
    return jax.shard_map(step, mesh=mesh, in_specs=in_specs, out_specs=out_specs, check_vma=False)
```

```python
import functools

import jax
import jax.numpy as jnp
from jax import lax
from jax.experimental import pallas as pl
from jax.experimental.pallas import tpu as pltpu
from jax.sharding import PartitionSpec as P

MESH = pl.DeviceIdType.MESH
LANES = 128
NEAR = ((0, 1), (0, -1), (1, 0), (-1, 0), (1, 1), (1, -1), (-1, 1), (-1, -1))
FAR = ((0, 2), (0, -2))


def run(count, step, most=8):
    unroll = max(k for k in range(1, most + 1) if count % k == 0)
    lax.fori_loop(0, count, step, 0, unroll=unroll)


def kernel(
    dims, feat_in, coef_in, k1_hbm, b1_in, k2_hbm, b2_in, out_ref,
    k1_in, k2_in, feat, coef, vol, hid, work, w1, w2, prep, bias, send_sem, recv_sem, local_sem,
):
    scenes, views, rows, planes, feats, groups, columns, regs, depth_n, rows_n = dims
    channels = groups + feats
    per_group = feats // groups
    packed = feat_in.shape[3]
    half = scenes // 2
    wide = 2 * LANES
    tail = columns - LANES
    d = lax.axis_index("depth")
    q = lax.axis_index("rows")
    side = lax.rem(d, 2)
    mate = d + 1 - 2 * side

    def exists(dd, dq):
        return (d + dd >= 0) & (d + dd < depth_n) & (q + dq >= 0) & (q + dq < rows_n)

    barrier = pltpu.get_barrier_semaphore()
    for dd, dq in NEAR + FAR:
        @pl.when(exists(dd, dq))
        def _():
            pl.semaphore_signal(barrier, inc=1, device_id=(d + dd, q + dq), device_id_type=MESH)

    taps = [
        pltpu.make_async_copy(k1_hbm, k1_in, local_sem.at[2]),
        pltpu.make_async_copy(k2_hbm, k2_in, local_sem.at[3]),
    ]
    local = [
        pltpu.make_async_copy(feat_in, feat.at[2], local_sem.at[0]),
        pltpu.make_async_copy(coef_in, coef.at[1, pl.ds(2, planes)], local_sem.at[1]),
    ]
    for copy in taps + local:
        copy.start()

    def feat_copy(dq, k):
        slot = 2 - dq
        count = views + 1 if abs(dq) == 1 else views
        return pltpu.make_async_remote_copy(
            src_ref=feat_in.at[pl.ds(side * half, half), pl.ds(0, count)],
            dst_ref=feat.at[slot, pl.ds(side * half, half), pl.ds(0, count)],
            send_sem=send_sem.at[k], recv_sem=recv_sem.at[k],
            device_id=(d, q + dq), device_id_type=MESH,
        )

    def mate_copy(dq, k):
        slot = 2 - dq
        count = views + 1 if abs(dq) == 1 else views
        part = feat.at[slot, pl.ds(side * half, half), pl.ds(0, count)]
        return pltpu.make_async_remote_copy(
            src_ref=part, dst_ref=part,
            send_sem=send_sem.at[k], recv_sem=recv_sem.at[k],
            device_id=(mate, q), device_id_type=MESH,
        )

    def coef_copy(dd, dq, k):
        if dd == 0:
            first, count, at = 0, planes, 2
        elif dd == 1:
            first, count, at = planes - 2, 2, 0
        else:
            first, count, at = 0, 2, planes + 2
        return pltpu.make_async_remote_copy(
            src_ref=coef_in.at[pl.ds(first, count)],
            dst_ref=coef.at[1 - dq, pl.ds(at, count)],
            send_sem=send_sem.at[k], recv_sem=recv_sem.at[k],
            device_id=(d + dd, q + dq), device_id_type=MESH,
        )

    near_feat = [((0, dq), feat_copy(dq, i)) for i, dq in enumerate((1, -1))]
    far_feat = [((0, dq), feat_copy(dq, 2 + i)) for i, dq in enumerate((2, -2))]
    depth_coef = [((dd, 0), coef_copy(dd, 0, 4 + i)) for i, dd in enumerate((1, -1))]
    side_coef = [
        ((dd, dq), coef_copy(dd, dq, 6 + i))
        for i, (dd, dq) in enumerate([m for m in NEAR if m[1] != 0])
    ]
    every = near_feat + depth_coef + far_feat + side_coef
    near_mate = [((0, dq), mate_copy(dq, 12 + i)) for i, dq in enumerate((1, -1))]
    far_mate = [((0, dq), mate_copy(dq, 14 + i)) for i, dq in enumerate((2, -2))]

    for slot, gone in ((0, q < 2), (1, q < 1), (3, q + 1 >= rows_n), (4, q + 2 >= rows_n)):
        @pl.when(gone)
        def _():
            feat[slot] = jnp.zeros(feat.shape[1:], feat.dtype)

    beside = 1 + lax.div(d + depth_n - 1, depth_n) + lax.div(2 * depth_n - 2 - d, depth_n)
    above = 1 + lax.div(q + rows_n - 1, rows_n) + lax.div(2 * rows_n - 2 - q, rows_n)
    beyond = lax.div(q + rows_n - 2, rows_n) + lax.div(2 * rows_n - 3 - q, rows_n)
    pl.semaphore_wait(barrier, beside * above - 1 + beyond)

    for (dd, dq), copy in every:
        @pl.when(exists(dd, dq))
        def _():
            copy.start()

    def arrive(pairs):
        for (dd, dq), copy in pairs:
            @pl.when(exists(-dd, -dq))
            def _():
                copy.wait_recv()

    def hand_on(pairs):
        for (dd, dq), copy in pairs:
            @pl.when(exists(-dd, -dq))
            def _():
                copy.start()

    def place(kernel_in, count, span, target, dest, order=None):
        for a in range(3):
            for r in range(3):
                line = jnp.zeros((regs, span), jnp.float32)
                for s in range(3):
                    c = lax.broadcasted_iota(jnp.int32, (count, span), 0)
                    k = lax.broadcasted_iota(jnp.int32, (count, span), 1)
                    pick = jnp.where(dest(s, c) == k, 1.0, 0.0).astype(jnp.bfloat16)
                    line = line + jnp.dot(kernel_in[a, r, s], pick, preferred_element_type=jnp.float32)
                line = line.astype(jnp.bfloat16)
                if order is not None:
                    line = jnp.dot(order, line, preferred_element_type=jnp.float32)
                    line = line.astype(jnp.bfloat16)
                for j in range(rows):
                    target[pl.ds((a * rows + j) * regs, regs), pl.ds((j + r) * span, span)] = line

    def first_dest(s, c):
        f = c - groups
        spread_at = s * feats + (f % per_group) * groups + f // per_group
        return jnp.where(c < groups, 3 * feats + s * groups + c, spread_at)

    w1[...] = jnp.zeros(w1.shape, w1.dtype)
    w2[...] = jnp.zeros(w2.shape, w2.dtype)
    for copy in taps:
        copy.wait()
    place(k1_in, channels, LANES, w1, first_dest)
    per_out = regs // groups
    at_row = lax.broadcasted_iota(jnp.int32, (regs, regs), 0)
    at_channel = lax.broadcasted_iota(jnp.int32, (regs, regs), 1)
    order = at_channel == (at_row % groups) * per_out + at_row // groups
    place(
        k2_in, regs, LANES, w2, lambda s, c: s * regs + c,
        jnp.where(order, 1.0, 0.0).astype(jnp.bfloat16),
    )
    for i, (b_in, mask) in enumerate(((b1_in, at_row == at_channel), (b2_in, order))):
        column = jnp.sum(jnp.where(mask, b_in[...], 0.0), axis=1, keepdims=True)
        bias[i] = jnp.broadcast_to(jnp.concatenate([column] * rows, axis=0), (rows * regs, wide))

    for copy in local:
        copy.wait()

    lane = lax.broadcasted_iota(jnp.int32, (groups, LANES), 1)
    in_tail = lane < tail

    def unpack(tail_packed):
        parts = []
        for j in range(per_group):
            part = tail_packed if j == 0 else pltpu.roll(tail_packed, LANES - tail * j, 1)
            parts.append(jnp.where(in_tail, part, 0.0))
        return parts

    def volume_rows(block):
        for b in range(scenes):
            for m in range(rows):
                ref = feat[block + 1, b, views, m].astype(jnp.float32)
                prep[3 * views] = ref
                for v in range(views):
                    low = feat[block, b, v, m].astype(jnp.float32)
                    mid = feat[block + 1, b, v, m].astype(jnp.float32)
                    up = feat[block + 2, b, v, m].astype(jnp.float32)
                    prep[v] = mid - ref
                    prep[views + v] = low - mid
                    prep[2 * views + v] = up - mid
                row = (block - 1) * rows + m
                row_ok = (q * rows + row >= 0) & (q * rows + row < rows_n * rows)

                def plane(p, carry):
                    at = d * planes + p - 2
                    ok = row_ok & (at >= 0) & (at < depth_n * planes)
                    weights = coef[block, p, b, m].astype(jnp.float32)
                    others = 1.0 - weights
                    total = None
                    for v in range(views):
                        cl = weights[v : v + 1]
                        cu = others[views + v : views + v + 1]
                        both = []
                        for lo, hi, l0 in ((0, feats, 0), (feats, packed, LANES)):
                            both.append(
                                prep[v, lo:hi]
                                + cl[:, l0 : l0 + LANES] * prep[views + v, lo:hi]
                                + cu[:, l0 : l0 + LANES] * prep[2 * views + v, lo:hi]
                            )
                        if total is None:
                            total = both
                            square = [u * u for u in both]
                        else:
                            total = [t + u for t, u in zip(total, both)]
                            square = [t + u * u for t, u in zip(square, both)]
                    share = 1.0 / (views + 1.0)
                    spread = [(s2 - t * t * share) * share for s2, t in zip(square, total)]
                    refs = [prep[3 * views, 0:feats], prep[3 * views, feats:packed]]
                    product = [r * (t + (1.0 * views) * r) for r, t in zip(refs, total)]
                    scale = 1.0 / (views * per_group)
                    head = product[0][0:groups]
                    for j in range(1, per_group):
                        head = head + product[0][j * groups : (j + 1) * groups]
                    rest = product[1]
                    step = LANES // 2
                    while step >= tail:
                        rest = rest + pltpu.roll(rest, step, 1)
                        step //= 2
                    corr = jnp.concatenate([head, jnp.where(in_tail, rest, 0.0)], axis=1) * scale
                    ends = unpack(spread[1])
                    full = jnp.concatenate(
                        [jnp.concatenate([spread[0], jnp.concatenate(ends, axis=0)], axis=1), corr],
                        axis=0,
                    )
                    full = jnp.where(ok, full, 0.0)
                    left = pltpu.roll(full, 1, 1)
                    right = pltpu.roll(full, wide - 1, 1)
                    lines = [left[:feats], full[:feats], right[:feats]]
                    lines += [left[feats:], full[feats:], right[feats:]]
                    lines.append(jnp.zeros((LANES - 3 * channels, wide), jnp.float32))
                    vol[b, p, row + rows] = jnp.concatenate(lines, axis=0).astype(jnp.bfloat16)
                    return carry

                run(planes + 4, plane)

    arrive(near_feat)
    hand_on(near_mate)
    arrive(depth_coef)
    arrive(near_mate)
    volume_rows(1)
    arrive(far_feat)
    hand_on(far_mate)

    size = rows * regs

    def products(own):
        for b in range(scenes):
            for pair in range(2):
                start = rows if own else 2 * rows * pair
                line = w1.at[:, pl.ds((start - pair * rows) * LANES, rows * LANES)]

                def first(p, carry):
                    piece = vol[b, p, pl.ds(start, rows)].reshape(rows * LANES, wide)
                    value = jnp.dot(line[...], piece, preferred_element_type=jnp.float32)
                    if not own:
                        value = value + work[2 * b + pair, p]
                    work[2 * b + pair, p] = value
                    return carry

                run(planes + 4, first)

    products(True)
    arrive(side_coef)
    arrive(far_mate)
    volume_rows(0)
    volume_rows(2)
    products(False)
    inside = lax.broadcasted_iota(jnp.int32, (regs, wide), 1) < columns
    for b in range(scenes):
        for pair in range(2):
            base = pair * rows
            at_work = work.at[2 * b + pair]

            def hidden(p, carry):
                summed = (
                    at_work[p, 0:size] + at_work[p + 1, size : 2 * size]
                    + at_work[p + 2, 2 * size : 3 * size] + bias[0]
                )
                summed = jnp.maximum(summed, 0.0)
                at = d * planes + p - 1
                for j in range(rows):
                    row = q * rows + base + j - 1
                    ok = (at >= 0) & (at < depth_n * planes) & (row >= 0) & (row < rows_n * rows)
                    part = summed[j * regs : (j + 1) * regs]
                    part = jnp.where(inside & ok, part, 0.0)
                    part = part.astype(jnp.bfloat16).astype(jnp.float32)
                    lines = [pltpu.roll(part, 1, 1), part, pltpu.roll(part, wide - 1, 1)]
                    lines.append(jnp.zeros((LANES - 3 * regs, wide), jnp.float32))
                    hid[b, p, base + j] = jnp.concatenate(lines, axis=0).astype(jnp.bfloat16)
                return carry

            run(planes + 2, hidden)

        def second(p, carry):
            piece = hid[b, p].reshape((rows + 2) * LANES, wide)
            work[0, p] = jnp.dot(w2[...], piece, preferred_element_type=jnp.float32)
            return carry

        run(planes + 2, second)

        def finish(p, carry):
            summed = (
                work[0, p, 0:size] + work[0, p + 1, size : 2 * size]
                + work[0, p + 2, 2 * size : 3 * size] + bias[1]
            )
            for j in range(rows):
                for t in range(per_out):
                    first_row = j * regs + t * groups
                    part = summed[first_row : first_row + groups, 0:columns]
                    out_ref[b, p, j, :, pl.ds(t * columns, columns)] = part.astype(jnp.bfloat16)
            return carry

        run(planes, finish)

    for (dd, dq), copy in every:
        @pl.when(exists(dd, dq))
        def _():
            copy.wait_send()

    for (dd, dq), copy in near_mate + far_mate:
        @pl.when(exists(-dd, -dq))
        def _():
            copy.wait_send()


def body(
    depth_n, rows_n, ref_feat, src_feat, block_index, blend, conv_first, bias_first, conv_second, bias_second
):
    scenes, views, rows, flat = src_feat.shape
    planes, columns = blend.shape[2], blend.shape[4]
    channels, regs = conv_first.shape[4], conv_first.shape[3]
    feats = flat // columns
    groups = channels - feats
    per_group = feats // groups
    tail = columns - LANES
    packed = feats + groups

    cube = jnp.concatenate([src_feat, ref_feat[:, None]], axis=1)
    cube = cube.reshape(scenes, views + 1, rows, groups, per_group, columns)
    main = jnp.moveaxis(cube[..., :LANES], 4, 3).reshape(scenes, views + 1, rows, feats, LANES)
    ends = cube[..., LANES:].reshape(scenes, views + 1, rows, groups, per_group * tail)
    feat_in = jnp.concatenate([main, ends], axis=3)

    below = (block_index < lax.axis_index("rows"))[:, :, :, :, None]
    lower = jnp.where(below, blend, jnp.zeros_like(blend))
    upper = jnp.where(below, jnp.ones_like(blend), blend)
    coef = jnp.concatenate([lower, upper], axis=1)
    coef = jnp.concatenate([coef[..., :LANES]] + [coef[..., LANES:]] * per_group, axis=4)
    coef_in = jnp.transpose(coef, (2, 0, 3, 1, 4))

    wide = 2 * LANES
    dims = (scenes, views, rows, planes, feats, groups, columns, regs, depth_n, rows_n)
    bf16, f32 = jnp.bfloat16, jnp.float32
    out = pl.pallas_call(
        functools.partial(kernel, dims),
        out_shape=jax.ShapeDtypeStruct((scenes, planes, rows, groups, regs // groups * columns), bf16),
        in_specs=[
            pl.BlockSpec(memory_space=pl.ANY),
            pl.BlockSpec(memory_space=pl.ANY),
            pl.BlockSpec(memory_space=pl.ANY),
            pl.BlockSpec(memory_space=pltpu.VMEM),
            pl.BlockSpec(memory_space=pl.ANY),
            pl.BlockSpec(memory_space=pltpu.VMEM),
        ],
        out_specs=pl.BlockSpec(memory_space=pltpu.VMEM),
        scratch_shapes=[
            pltpu.VMEM(conv_first.shape, bf16),
            pltpu.VMEM(conv_second.shape, bf16),
            pltpu.VMEM((5, scenes, views + 1, rows, packed, LANES), bf16),
            pltpu.VMEM((3, planes + 4, scenes, rows, 2 * views, wide), bf16),
            pltpu.VMEM((scenes, planes + 4, 3 * rows, LANES, wide), bf16),
            pltpu.VMEM((scenes, planes + 2, rows + 2, LANES, wide), bf16),
            pltpu.VMEM((2 * scenes, planes + 4, 3 * rows * regs, wide), f32),
            pltpu.VMEM((3 * rows * regs, (rows + 2) * LANES), bf16),
            pltpu.VMEM((3 * rows * regs, (rows + 2) * LANES), bf16),
            pltpu.VMEM((3 * views + 1, packed, LANES), f32),
            pltpu.VMEM((2, rows * regs, wide), f32),
            pltpu.SemaphoreType.DMA((16,)),
            pltpu.SemaphoreType.DMA((16,)),
            pltpu.SemaphoreType.DMA((4,)),
        ],
        compiler_params=pltpu.CompilerParams(
            collective_id=0, has_side_effects=True, vmem_limit_bytes=56 << 20
        ),
    )(feat_in, coef_in, conv_first, bias_first[None], conv_second, bias_second[None])
    return out.reshape(scenes, planes, rows, regs * columns)


def solution(mesh):
    in_specs = (
        P(None, "rows", None),
        P(None, None, "rows", None),
        P(None, None, "depth", "rows"),
        P(None, None, "depth", "rows", None),
        P(),
        P(),
        P(),
        P(),
    )
    out_specs = P(None, "depth", "rows", None)
    step = functools.partial(body, mesh.shape["depth"], mesh.shape["rows"])
    return jax.shard_map(step, mesh=mesh, in_specs=in_specs, out_specs=out_specs, check_vma=False)
```
